32 devices in a mesh: groups: 2 (over y), tm: 4 (over z), chan: 2 (over x), sub: 2 (over core).
Axes of the slice: x: 2, y: 2, z: 4, core: 2. Of those that a mesh axis runs over, the one named last changes fastest.
Arguments:
- traces: bfloat16 [512, 8192], P(('chan', 'sub'), ('groups', 'tm')), parts along dimension 1, may hold values from -60 to 60
- templates: bfloat16 [32, 512, 256], P('tm', ('chan', 'sub')), may hold values from -6 to 6
- channel_mask: int32 [32, 512], P('tm', ('chan', 'sub')), may hold values from 0 to 1
Outputs:
- scores: float32 [32, 8192], P(('chan', 'sub'), ('groups', 'tm')), parts along dimension 1
The draws below stay inside these ranges and needn't reach their ends.
There are 2 independent parts, one for each index of `groups`. The reference program is written for one: setup_inputs(seed, part) draws one part's arguments, and reference() takes and returns one part's arrays. A program takes and returns all parts, laid end to end along the dimension named above; an argument that names none is the same for every part. Nothing has to cross between parts.
All inputs are finite; a program needn't handle non-finite values.
Results may differ from the reference program's by a relative error of at most 0.0003.
Values may be sent and summed in bfloat16 or wider, within the bound.
A program may use at most 64 MiB of HBM per device.

```python
import jax
import jax.numpy as jnp
from jax import lax

S = 256
TEMPLATES = 32
CHANNELS = 512
TIME = 4096


def draw_traces(key, part):
    scale_key, envelope_key, noise_key = jax.random.split(key, 3)
    chan_scale = jnp.exp(jax.random.uniform(scale_key, (CHANNELS, 1), jnp.float32, 0.0, 2.3))
    envelope = jnp.exp(jax.random.uniform(envelope_key, (1, TIME // 64), jnp.float32, -0.7, 0.7))
    envelope = jnp.repeat(envelope, 64, axis=1)
    noise = jax.random.normal(noise_key, (CHANNELS, TIME), jnp.float32)
    values = jnp.clip(noise * chan_scale * envelope, -60.0, 60.0)
    return values.astype(jnp.bfloat16)


def mask_pattern(key):
    mask_key, drop_key = jax.random.split(jax.random.fold_in(key, 7))
    used = jax.random.randint(mask_key, (TEMPLATES, CHANNELS), 0, 2, jnp.int32)
    dropped = jax.random.randint(drop_key, (TEMPLATES, CHANNELS), 0, 16, jnp.int32)
    silent = used * (dropped == 0).astype(jnp.int32)
    return (used, silent)


def draw_channel_mask(key, part):
    used, silent = mask_pattern(key)
    return used


def draw_templates(key, part):
    used, silent = mask_pattern(key)
    wave_key = jax.random.fold_in(key, 11)
    values = jnp.clip(jax.random.normal(wave_key, (TEMPLATES, CHANNELS, S), jnp.float32), -6.0, 6.0)
    keep = (1 - silent).astype(jnp.float32)[:, :, None]
    return (values * keep).astype(jnp.bfloat16)


def setup_inputs(seed: int = 0, part: int = 0) -> dict:
    arg_keys = jax.random.split(jax.random.key(seed), 4)
    part_splits = jax.random.split(jax.random.fold_in(arg_keys[3], part), 4)
    return {
        "traces": draw_traces(jax.random.fold_in(jax.random.fold_in(arg_keys[3], part), 71), part),
        "templates": draw_templates(jax.random.fold_in(arg_keys[3], 71), part),
        "channel_mask": draw_channel_mask(jax.random.fold_in(arg_keys[3], 71), part),
    }


EPSILON = 1e-06

def reference(traces, templates, channel_mask):
    signal = traces.astype(jnp.float32)
    wrapped = jnp.concatenate([signal, signal[:, :S]], 1)
    squares = wrapped * wrapped
    masked = templates * channel_mask.astype(jnp.bfloat16)[:, :, None]
    weights = masked.astype(jnp.float32)

    def advance(state_tuple, offset):
        correlation, chan_energy = state_tuple
        window = lax.dynamic_slice_in_dim(wrapped, offset, TIME, 1)
        lag_weights = lax.dynamic_index_in_dim(weights, offset, 2, keepdims=False)
        correlation = correlation + jnp.dot(lag_weights, window, precision=lax.Precision.HIGHEST, preferred_element_type=jnp.float32)
        chan_energy = chan_energy + lax.dynamic_slice_in_dim(squares, offset, TIME, 1)
        return ((correlation, chan_energy), None)
    initial = (jnp.zeros((TEMPLATES, TIME), jnp.float32), jnp.zeros((CHANNELS, TIME), jnp.float32))
    (correlation, chan_energy), _ = lax.scan(advance, initial, jnp.arange(S, dtype=jnp.int32))
    active = channel_mask.astype(jnp.float32)
    template_energy = lax.optimization_barrier(jnp.sum(weights * weights, axis=(1, 2)))
    active_count = lax.optimization_barrier(jnp.sum(active, axis=1))
    energy = jnp.dot(active, chan_energy, precision=lax.Precision.HIGHEST, preferred_element_type=jnp.float32)
    factor = jnp.sqrt(S * active_count)[:, None]
    return correlation * factor / jnp.sqrt(energy * template_energy[:, None] + EPSILON)
```

```python
import functools

import jax
import jax.numpy as jnp
from jax import lax
from jax.experimental import pallas as pl
from jax.experimental.pallas import tpu as pltpu
from jax.sharding import PartitionSpec as P

EPSILON = 1e-06
MESH = pl.DeviceIdType.MESH
LANES = 128
FRAMES = 4
FINE = LANES // FRAMES


def kernel(sizes, x_ref, w_ref, m_ref, o_ref, xb, af, ab, fr, pr, st, tb, rb,
           recv_sem, right_sem, left_sem, out_sem, in_sem):
    tm, chan_n, sub_n = sizes
    cs_n = chan_n * sub_n
    me = lax.axis_index("tm")
    my_chan = lax.axis_index("chan")
    my_sub = lax.axis_index("sub")
    my_cs = my_chan * sub_n + my_sub
    chans, tile = x_ref.shape
    rows, _, span = w_ref.shape
    blocks = tm // cs_n
    coarse = span // FINE
    wide = tile + LANES
    owner = me // blocks
    owner_chan = owner // sub_n
    owner_sub = owner % sub_n

    barrier = pltpu.get_barrier_semaphore()
    count = 0
    for a in range(tm):
        for b in range(chan_n):
            for c in range(sub_n):
                if a or b or c:
                    pl.semaphore_signal(
                        barrier, inc=1,
                        device_id={"tm": lax.rem(me + a, tm),
                                   "chan": lax.rem(my_chan + b, chan_n),
                                   "sub": lax.rem(my_sub + c, sub_n)},
                        device_id_type=MESH)
                    count += 1
    pl.semaphore_wait(barrier, count)

    def relay(src, index, to, sem):
        return pltpu.make_async_remote_copy(
            src_ref=src, dst_ref=xb.at[index], send_sem=sem.at[index],
            recv_sem=recv_sem.at[index], device_id={"tm": to}, device_id_type=MESH)

    @pl.when(me < tm - 1)
    def _():
        relay(x_ref, me, me + 1, right_sem).start()

    @pl.when(me > 0)
    def _():
        relay(x_ref, me, me - 1, left_sem).start()

    xb[me] = x_ref[...]

    mask = m_ref[...].astype(jnp.float32)
    for k in range(rows):
        wave = jnp.transpose(w_ref[k].astype(jnp.float32)) * mask[k : k + 1, :]
        tb[k : k + 1, :] = jnp.sum(wave * wave, axis=0, keepdims=True)
        for g in range(coarse):
            af[g, pl.ds(k, FINE, stride=rows), :] = wave[g * FINE : (g + 1) * FINE, :]
    for g in range(coarse):
        ab[:, g * chans : (g + 1) * chans] = af[g].astype(jnp.bfloat16)
    mask_bf = mask.astype(jnp.bfloat16)
    mask_two = jnp.concatenate([mask_bf, mask_bf], 1)
    local_slot = (me % blocks) * cs_n + my_cs

    def result_copy(t):
        return pltpu.make_async_remote_copy(
            src_ref=st.at[t], dst_ref=rb.at[local_slot], send_sem=out_sem.at[t],
            recv_sem=in_sem.at[local_slot],
            device_id={"tm": t, "chan": owner_chan, "sub": owner_sub}, device_id_type=MESH)

    def process(t):
        after = lax.rem(t + 1, tm)
        ext = jnp.concatenate([xb[t], xb[after, :, : span + LANES]], 1)
        for f in range(FRAMES):
            moved = ext[:, f * FINE : f * FINE + tile + span]
            for h in range(span // LANES):
                g = h * FRAMES + f
                fr[g * chans : (g + 1) * chans, :] = moved[:, h * LANES : h * LANES + wide]
        pr[...] = jnp.dot(ab[...], fr[...], preferred_element_type=jnp.float32)
        corr = pr[0:rows, :tile]
        for b in range(1, FINE):
            corr = corr + pltpu.roll(pr[b * rows : (b + 1) * rows, :], wide - b, 1)[:, :tile]
        x32 = ext[:, : tile + span].astype(jnp.float32)
        square = x32 * x32
        high = square.astype(jnp.bfloat16)
        low = (square - high.astype(jnp.float32)).astype(jnp.bfloat16)
        power = jnp.dot(mask_two, jnp.concatenate([high, low], 0),
                        preferred_element_type=jnp.float32)
        by = 1
        while by < span:
            power = power + pltpu.roll(power, tile + span - by, 1)
            by *= 2
        power = power[:, :tile]
        own = jnp.logical_and(t == me, my_cs == owner)

        @pl.when(own)
        def _():
            rb[local_slot, 0:rows, 0:tile] = corr
            rb[local_slot, rows : 2 * rows, 0:tile] = power
            rb[local_slot, 0:rows, tile:] = tb[...]
            rb[local_slot, rows : 2 * rows, tile:] = mask

        @pl.when(jnp.logical_not(own))
        def _():
            st[t, 0:rows, 0:tile] = corr
            st[t, rows : 2 * rows, 0:tile] = power
            st[t, 0:rows, tile:] = tb[...]
            st[t, rows : 2 * rows, tile:] = mask
            result_copy(t).start()

    def step(u, carry):
        i = u // 2
        right_side = u % 2 == 0
        last = u == 2 * (tm - 1)
        from_left = me - 1 - i
        from_right = me + 1 + i
        first = jnp.logical_and(right_side, jnp.logical_not(last))

        @pl.when(jnp.logical_and(first, from_left >= 0))
        def _():
            relay(x_ref, from_left, me, right_sem).wait_recv()

            @pl.when(me < tm - 1)
            def _():
                relay(xb.at[from_left], from_left, me + 1, right_sem).start()

        @pl.when(jnp.logical_and(first, from_right <= tm - 1))
        def _():
            relay(x_ref, from_right, me, left_sem).wait_recv()

            @pl.when(me > 0)
            def _():
                relay(xb.at[from_right], from_right, me - 1, left_sem).start()

        t = jnp.where(last, tm - 1, jnp.where(right_side, me + i, from_left))
        valid = jnp.logical_or(
            last, jnp.logical_or(jnp.logical_and(right_side, from_right <= tm - 1),
                                 jnp.logical_and(jnp.logical_not(right_side), from_left >= 0)))

        @pl.when(valid)
        def _():
            process(t)

        return carry

    lax.fori_loop(0, 2 * (tm - 1) + 1, step, 0)

    def finish(t, carry):
        @pl.when(jnp.logical_and(me < tm - 1, t <= me))
        def _():
            relay(x_ref, t, me, right_sem).wait_send()

        @pl.when(jnp.logical_and(me > 0, t >= me))
        def _():
            relay(x_ref, t, me, left_sem).wait_send()

        @pl.when(jnp.logical_not(jnp.logical_and(t == me, my_cs == owner)))
        def _():
            result_copy(t).wait_send()

        return carry

    lax.fori_loop(0, tm, finish, 0)

    for q in range(blocks):
        for c in range(cs_n):
            slot = q * cs_n + c
            mine = jnp.logical_and(my_cs == owner, slot == local_slot)

            @pl.when(jnp.logical_not(mine))
            def _():
                pltpu.make_async_remote_copy(
                    src_ref=st.at[0], dst_ref=rb.at[slot], send_sem=out_sem.at[0],
                    recv_sem=in_sem.at[slot],
                    device_id={"tm": me}, device_id_type=MESH).wait_recv()

    for q in range(blocks):
        total = rb[q * cs_n]
        for c in range(1, cs_n):
            total = total + rb[q * cs_n + c]
        te = jnp.sum(total[0:rows, tile:], axis=1, keepdims=True)
        active = jnp.sum(total[rows : 2 * rows, tile:], axis=1, keepdims=True)
        factor = jnp.sqrt(span * active)
        o_ref[q * rows : (q + 1) * rows, :] = (
            total[0:rows, :tile] * factor
            / jnp.sqrt(total[rows : 2 * rows, :tile] * te + EPSILON))


def solution(mesh):
    tm, chan_n, sub_n = (mesh.shape[a] for a in ("tm", "chan", "sub"))
    cs_n = chan_n * sub_n
    blocks = tm // cs_n

    def on_device(traces, templates, channel_mask):
        chans, tile = traces.shape
        rows, _, span = templates.shape
        coarse = span // FINE
        wide = tile + LANES
        vmem = pl.BlockSpec(memory_space=pltpu.VMEM)
        return pl.pallas_call(
            functools.partial(kernel, (tm, chan_n, sub_n)),
            out_shape=jax.ShapeDtypeStruct((blocks * rows, tile), jnp.float32),
            in_specs=[vmem] * 3,
            out_specs=vmem,
            scratch_shapes=[
                pltpu.VMEM((tm, chans, tile), jnp.bfloat16),
                pltpu.VMEM((coarse, FINE * rows, chans), jnp.float32),
                pltpu.VMEM((FINE * rows, coarse * chans), jnp.bfloat16),
                pltpu.VMEM((coarse * chans, wide), jnp.bfloat16),
                pltpu.VMEM((FINE * rows, wide), jnp.float32),
                pltpu.VMEM((tm, 2 * rows, wide), jnp.float32),
                pltpu.VMEM((rows, chans), jnp.float32),
                pltpu.VMEM((blocks * cs_n, 2 * rows, wide), jnp.float32),
                pltpu.SemaphoreType.DMA((tm,)),
                pltpu.SemaphoreType.DMA((tm,)),
                pltpu.SemaphoreType.DMA((tm,)),
                pltpu.SemaphoreType.DMA((tm,)),
                pltpu.SemaphoreType.DMA((blocks * cs_n,)),
            ],
            compiler_params=pltpu.CompilerParams(collective_id=0, has_side_effects=True),
        )(traces, templates, channel_mask)

    placed = (
        P(("chan", "sub"), ("groups", "tm")),
        P("tm", ("chan", "sub"), None),
        P("tm", ("chan", "sub")),
    )
    return jax.shard_map(
        on_device,
        mesh=mesh,
        in_specs=placed,
        out_specs=P(("chan", "sub"), ("groups", "tm")),
        check_vma=False,
    )
```

```python
import functools

import jax
import jax.numpy as jnp
from jax import lax
from jax.experimental import pallas as pl
from jax.experimental.pallas import tpu as pltpu
from jax.sharding import PartitionSpec as P

EPSILON = 1e-06
MESH = pl.DeviceIdType.MESH
LANES = 128
FRAMES = 4
FINE = LANES // FRAMES
PIECES = 2


def kernel(sizes, x_ref, w_ref, m_ref, o_ref, xb, af, ab, fr, pr, st, tb, rb, fin, ob,
           recv_sem, right_sem, left_sem, out_sem, in_sem, score_sem, done_sem):
    tm, chan_n, sub_n = sizes
    cs_n = chan_n * sub_n
    me = lax.axis_index("tm")
    my_chan = lax.axis_index("chan")
    my_sub = lax.axis_index("sub")
    my_cs = my_chan * sub_n + my_sub
    chans, tile = x_ref.shape
    rows, _, span = w_ref.shape
    blocks = tm // cs_n
    coarse = span // FINE
    wide = tile + LANES
    part = chans // PIECES
    owner = me // blocks

    barrier = pltpu.get_barrier_semaphore()

    @pl.when(me < tm - 1)
    def _():
        pl.semaphore_signal(barrier, inc=1, device_id={"tm": me + 1}, device_id_type=MESH)

    @pl.when(me > 0)
    def _():
        pl.semaphore_signal(barrier, inc=1, device_id={"tm": me - 1}, device_id_type=MESH)

    for b in range(chan_n):
        for c in range(sub_n):
            if b or c:
                pl.semaphore_signal(
                    barrier, inc=1,
                    device_id={"chan": lax.rem(my_chan + b, chan_n),
                               "sub": lax.rem(my_sub + c, sub_n)},
                    device_id_type=MESH)

    xb[me] = x_ref[...]
    mask = m_ref[...].astype(jnp.float32)
    for k in range(rows):
        wave = jnp.transpose(w_ref[k].astype(jnp.float32)) * mask[k : k + 1, :]
        tb[k : k + 1, :] = jnp.sum(wave * wave, axis=0, keepdims=True)
        for g in range(coarse):
            af[g, pl.ds(k, FINE, stride=rows), :] = wave[g * FINE : (g + 1) * FINE, :]
    for g in range(coarse):
        ab[:, g * chans : (g + 1) * chans] = af[g].astype(jnp.bfloat16)
    mask_bf = mask.astype(jnp.bfloat16)
    mask_two = jnp.concatenate([mask_bf, mask_bf], 1)

    at_end = jnp.logical_or(me == 0, me == tm - 1)
    pl.semaphore_wait(barrier, cs_n - 1 + jnp.where(at_end, 1, 2))

    def relay(src, index, p, to, sem):
        rows_of = pl.ds(p * part, part)
        return pltpu.make_async_remote_copy(
            src_ref=src.at[rows_of], dst_ref=xb.at[index, rows_of], send_sem=sem.at[index, p],
            recv_sem=recv_sem.at[index, p], device_id={"tm": to}, device_id_type=MESH)

    for p in range(PIECES):
        @pl.when(me < tm - 1)
        def _():
            relay(x_ref, me, p, me + 1, right_sem).start()

        @pl.when(me > 0)
        def _():
            relay(x_ref, me, p, me - 1, left_sem).start()

    def sum_copy(t):
        at = t % cs_n
        slot = (t // cs_n) * cs_n + my_cs
        return pltpu.make_async_remote_copy(
            src_ref=st.at[t], dst_ref=rb.at[slot], send_sem=out_sem.at[t],
            recv_sem=in_sem.at[slot],
            device_id={"chan": at // sub_n, "sub": at % sub_n}, device_id_type=MESH)

    def score_copy(q):
        return pltpu.make_async_remote_copy(
            src_ref=fin.at[q], dst_ref=ob.at[me % blocks], send_sem=score_sem.at[q],
            recv_sem=done_sem.at[me % blocks],
            device_id={"tm": q * cs_n + my_cs, "chan": owner // sub_n, "sub": owner % sub_n},
            device_id_type=MESH)

    def process(t):
        after = lax.rem(t + 1, tm)
        ext = jnp.concatenate([xb[t], xb[after, :, : span + LANES]], 1)
        for f in range(FRAMES):
            moved = ext[:, f * FINE : f * FINE + tile + span]
            for h in range(span // LANES):
                g = h * FRAMES + f
                fr[g * chans : (g + 1) * chans, :] = moved[:, h * LANES : h * LANES + wide]
        pr[...] = jnp.dot(ab[...], fr[...], preferred_element_type=jnp.float32)
        corr = pr[0:rows, :tile]
        for b in range(1, FINE):
            corr = corr + pltpu.roll(pr[b * rows : (b + 1) * rows, :], wide - b, 1)[:, :tile]
        x32 = ext[:, : tile + span].astype(jnp.float32)
        square = x32 * x32
        high = square.astype(jnp.bfloat16)
        low = (square - high.astype(jnp.float32)).astype(jnp.bfloat16)
        power = jnp.dot(mask_two, jnp.concatenate([high, low], 0),
                        preferred_element_type=jnp.float32)
        by = 1
        while by < span:
            power = power + pltpu.roll(power, tile + span - by, 1)
            by *= 2
        power = power[:, :tile]

        def put(ref, index):
            ref[index, 0:rows, 0:tile] = corr
            ref[index, rows : 2 * rows, 0:tile] = power
            ref[index, 0:rows, tile:] = tb[...]
            ref[index, rows : 2 * rows, tile:] = mask

        own = t % cs_n == my_cs

        @pl.when(own)
        def _():
            put(rb, (t // cs_n) * cs_n + my_cs)

        @pl.when(jnp.logical_not(own))
        def _():
            put(st, t)
            sum_copy(t).start()

    def step(u, carry):
        i = u // 2
        right_side = u % 2 == 0
        last = u == 2 * (tm - 1)
        from_left = me - 1 - i
        from_right = me + 1 + i
        first = jnp.logical_and(right_side, jnp.logical_not(last))

        for p in range(PIECES):
            @pl.when(jnp.logical_and(first, from_left >= 0))
            def _():
                relay(x_ref, from_left, p, me, right_sem).wait_recv()

                @pl.when(me < tm - 1)
                def _():
                    relay(xb.at[from_left], from_left, p, me + 1, right_sem).start()

            @pl.when(jnp.logical_and(first, from_right <= tm - 1))
            def _():
                relay(x_ref, from_right, p, me, left_sem).wait_recv()

                @pl.when(me > 0)
                def _():
                    relay(xb.at[from_right], from_right, p, me - 1, left_sem).start()

        t = jnp.where(last, tm - 1, jnp.where(right_side, me + i, from_left))
        valid = jnp.logical_or(
            last, jnp.logical_or(jnp.logical_and(right_side, from_right <= tm - 1),
                                 jnp.logical_and(jnp.logical_not(right_side), from_left >= 0)))

        @pl.when(valid)
        def _():
            process(t)

        return carry

    lax.fori_loop(0, 2 * (tm - 1) + 1, step, 0)

    for q in range(blocks):
        t = q * cs_n + my_cs
        for c in range(cs_n):
            @pl.when(my_cs != c)
            def _():
                pltpu.make_async_remote_copy(
                    src_ref=st.at[0], dst_ref=rb.at[q * cs_n + c], send_sem=out_sem.at[0],
                    recv_sem=in_sem.at[q * cs_n + c],
                    device_id={"tm": me}, device_id_type=MESH).wait_recv()
        total = rb[q * cs_n]
        for c in range(1, cs_n):
            total = total + rb[q * cs_n + c]
        te = jnp.sum(total[0:rows, tile:], axis=1, keepdims=True)
        active = jnp.sum(total[rows : 2 * rows, tile:], axis=1, keepdims=True)
        factor = jnp.sqrt(span * active)
        scores = (total[0:rows, :tile] * factor
                  / jnp.sqrt(total[rows : 2 * rows, :tile] * te + EPSILON))
        here = jnp.logical_and(t == me, my_cs == owner)

        @pl.when(here)
        def _():
            ob[me % blocks] = scores

        @pl.when(jnp.logical_not(here))
        def _():
            fin[q] = scores
            score_copy(q).start()

    def finish(t, carry):
        for p in range(PIECES):
            @pl.when(jnp.logical_and(me < tm - 1, t <= me))
            def _():
                relay(x_ref, t, p, me, right_sem).wait_send()

            @pl.when(jnp.logical_and(me > 0, t >= me))
            def _():
                relay(x_ref, t, p, me, left_sem).wait_send()

        @pl.when(t % cs_n != my_cs)
        def _():
            sum_copy(t).wait_send()

        return carry

    lax.fori_loop(0, tm, finish, 0)

    for q in range(blocks):
        here = jnp.logical_and(q * cs_n + my_cs == me, my_cs == owner)

        @pl.when(jnp.logical_not(here))
        def _():
            score_copy(q).wait_send()

    for q in range(blocks):
        here = jnp.logical_and(my_cs * blocks + q == me, me % cs_n == my_cs)

        @pl.when(jnp.logical_not(here))
        def _():
            pltpu.make_async_remote_copy(
                src_ref=fin.at[0], dst_ref=ob.at[q], send_sem=score_sem.at[0],
                recv_sem=done_sem.at[q],
                device_id={"tm": me}, device_id_type=MESH).wait_recv()
        o_ref[q * rows : (q + 1) * rows, :] = ob[q]


def solution(mesh):
    tm, chan_n, sub_n = (mesh.shape[a] for a in ("tm", "chan", "sub"))
    cs_n = chan_n * sub_n
    blocks = tm // cs_n

    def on_device(traces, templates, channel_mask):
        chans, tile = traces.shape
        rows, _, span = templates.shape
        coarse = span // FINE
        wide = tile + LANES
        vmem = pl.BlockSpec(memory_space=pltpu.VMEM)
        return pl.pallas_call(
            functools.partial(kernel, (tm, chan_n, sub_n)),
            out_shape=jax.ShapeDtypeStruct((blocks * rows, tile), jnp.float32),
            in_specs=[vmem] * 3,
            out_specs=vmem,
            scratch_shapes=[
                pltpu.VMEM((tm, chans, tile), jnp.bfloat16),
                pltpu.VMEM((coarse, FINE * rows, chans), jnp.float32),
                pltpu.VMEM((FINE * rows, coarse * chans), jnp.bfloat16),
                pltpu.VMEM((coarse * chans, wide), jnp.bfloat16),
                pltpu.VMEM((FINE * rows, wide), jnp.float32),
                pltpu.VMEM((tm, 2 * rows, wide), jnp.float32),
                pltpu.VMEM((rows, chans), jnp.float32),
                pltpu.VMEM((blocks * cs_n, 2 * rows, wide), jnp.float32),
                pltpu.VMEM((blocks, rows, tile), jnp.float32),
                pltpu.VMEM((blocks, rows, tile), jnp.float32),
                pltpu.SemaphoreType.DMA((tm, PIECES)),
                pltpu.SemaphoreType.DMA((tm, PIECES)),
                pltpu.SemaphoreType.DMA((tm, PIECES)),
                pltpu.SemaphoreType.DMA((tm,)),
                pltpu.SemaphoreType.DMA((blocks * cs_n,)),
                pltpu.SemaphoreType.DMA((blocks,)),
                pltpu.SemaphoreType.DMA((blocks,)),
            ],
            compiler_params=pltpu.CompilerParams(collective_id=0, has_side_effects=True),
        )(traces, templates, channel_mask)

    placed = (
        P(("chan", "sub"), ("groups", "tm")),
        P("tm", ("chan", "sub"), None),
        P("tm", ("chan", "sub")),
    )
    return jax.shard_map(
        on_device,
        mesh=mesh,
        in_specs=placed,
        out_specs=P(("chan", "sub"), ("groups", "tm")),
        check_vma=False,
    )
```

```python
import functools

import jax
import jax.numpy as jnp
from jax import lax
from jax.experimental import pallas as pl
from jax.experimental.pallas import tpu as pltpu
from jax.sharding import PartitionSpec as P

EPSILON = 1e-06
MESH = pl.DeviceIdType.MESH
LANES = 128
FRAMES = 4
FINE = LANES // FRAMES
PIECES = 2


def kernel(sizes, x_ref, w_ref, m_ref, o_ref, xb, af, ab, fr, pr, st, tb, rb, fin, ob, wx, mx,
           recv_sem, right_sem, left_sem, out_sem, in_sem, score_sem, done_sem,
           wave_out, wave_in, swap_out, mask_out, mask_in):
    group_n, tm, chan_n, sub_n = sizes
    group = lax.axis_index("groups")
    cs_n = chan_n * sub_n
    me = lax.axis_index("tm")
    my_chan = lax.axis_index("chan")
    my_sub = lax.axis_index("sub")
    my_cs = my_chan * sub_n + my_sub
    chans, tile = x_ref.shape
    rows, _, span = w_ref.shape
    blocks = tm // cs_n
    coarse = span // FINE
    wide = tile + LANES
    part = chans // PIECES
    owner = me // blocks
    share = rows // group_n
    my_at = my_sub * chan_n + my_chan
    is_end = jnp.logical_or(me == 0, me == tm - 1)
    is_helper = jnp.logical_or(me == 1, me == tm - 2)
    inner = jnp.where(me == 0, 1, tm - 2)
    extra_block = jnp.where(me == 1, 0, tm - 1)
    extra_tile = jnp.where(me == 1, tm - 1, 0)

    def skipped(t):
        return jnp.logical_or(jnp.logical_and(me == 0, t == tm - 1),
                              jnp.logical_and(me == tm - 1, t == 0))

    def place(t):
        at = t % cs_n
        return at % chan_n, at // chan_n

    barrier = pltpu.get_barrier_semaphore()

    @pl.when(me < tm - 1)
    def _():
        pl.semaphore_signal(barrier, inc=1, device_id={"tm": me + 1}, device_id_type=MESH)

    @pl.when(me > 0)
    def _():
        pl.semaphore_signal(barrier, inc=1, device_id={"tm": me - 1}, device_id_type=MESH)

    for b in range(chan_n):
        for c in range(sub_n):
            if b or c:
                pl.semaphore_signal(
                    barrier, inc=1,
                    device_id={"chan": lax.rem(my_chan + b, chan_n),
                               "sub": lax.rem(my_sub + c, sub_n)},
                    device_id_type=MESH)

    for d in range(1, group_n):
        pl.semaphore_signal(barrier, inc=1,
                            device_id={"groups": lax.rem(group + d, group_n)},
                            device_id_type=MESH)

    xb[me] = x_ref[...]

    def prepare(waves, used):
        mask = used[...].astype(jnp.float32)
        for k in range(rows):
            wave = jnp.transpose(waves[k].astype(jnp.float32)) * mask[k : k + 1, :]
            tb[k : k + 1, :] = jnp.sum(wave * wave, axis=0, keepdims=True)
            for g in range(coarse):
                af[g, pl.ds(k, FINE, stride=rows), :] = wave[g * FINE : (g + 1) * FINE, :]
        for g in range(coarse):
            ab[:, g * chans : (g + 1) * chans] = af[g].astype(jnp.bfloat16)

    prepare(w_ref, m_ref)

    pl.semaphore_wait(barrier, cs_n - 1 + group_n - 1 + jnp.where(is_end, 1, 2))

    def relay(method, src, index, p, to, sem, when):
        rightward = sem is right_sem
        far = jnp.logical_and(to == tm - 1, index == 0) if rightward else jnp.logical_and(
            to == 0, index == tm - 1)
        rows_of = pl.ds(p * part, part)
        for short in (False, True):
            columns = pl.ds(0, span if short else tile)

            @pl.when(jnp.logical_and(when, far if short else jnp.logical_not(far)))
            def _():
                getattr(pltpu.make_async_remote_copy(
                    src_ref=src.at[rows_of, columns], dst_ref=xb.at[index, rows_of, columns],
                    send_sem=sem.at[index, p], recv_sem=recv_sem.at[index, p],
                    device_id={"tm": to}, device_id_type=MESH), method)()

    for p in range(PIECES):
        relay("start", x_ref, me, p, me + 1, right_sem, me < tm - 1)
        relay("start", x_ref, me, p, me - 1, left_sem, me > 0)

    def wave_copy(k):
        return pltpu.make_async_remote_copy(
            src_ref=w_ref.at[k], dst_ref=wx.at[k], send_sem=wave_out.at[k],
            recv_sem=wave_in.at[k], device_id={"tm": inner}, device_id_type=MESH)

    def swap_copy(k, d):
        return pltpu.make_async_remote_copy(
            src_ref=wx.at[k], dst_ref=wx.at[k], send_sem=swap_out.at[d - 1, k],
            recv_sem=wave_in.at[k], device_id={"groups": lax.rem(group + d, group_n)},
            device_id_type=MESH)

    def mask_copy():
        return pltpu.make_async_remote_copy(
            src_ref=m_ref, dst_ref=mx, send_sem=mask_out, recv_sem=mask_in,
            device_id={"tm": inner}, device_id_type=MESH)

    @pl.when(is_end)
    def _():
        mask_copy().start()
        for k in range(share):
            wave_copy(group * share + k).start()

    def sum_copy(t):
        slot = (t // cs_n) * cs_n + my_cs
        to_chan, to_sub = place(t)
        return pltpu.make_async_remote_copy(
            src_ref=st.at[t], dst_ref=rb.at[slot], send_sem=out_sem.at[t],
            recv_sem=in_sem.at[slot],
            device_id={"chan": to_chan, "sub": to_sub}, device_id_type=MESH)

    def extra_copy():
        slot = blocks * cs_n + my_cs
        to_chan, to_sub = place(extra_tile)
        return pltpu.make_async_remote_copy(
            src_ref=st.at[tm], dst_ref=rb.at[slot], send_sem=out_sem.at[tm],
            recv_sem=in_sem.at[slot],
            device_id={"chan": to_chan, "sub": to_sub}, device_id_type=MESH)

    def score_copy(q):
        return pltpu.make_async_remote_copy(
            src_ref=fin.at[q], dst_ref=ob.at[me % blocks], send_sem=score_sem.at[q],
            recv_sem=done_sem.at[me % blocks],
            device_id={"tm": q * cs_n + my_at, "chan": owner // sub_n, "sub": owner % sub_n},
            device_id_type=MESH)

    def extra_score_copy():
        to = extra_block // blocks
        return pltpu.make_async_remote_copy(
            src_ref=fin.at[blocks], dst_ref=ob.at[extra_block % blocks],
            send_sem=score_sem.at[blocks], recv_sem=done_sem.at[extra_block % blocks],
            device_id={"tm": extra_tile, "chan": to // sub_n, "sub": to % sub_n},
            device_id_type=MESH)

    def process(t, used, extra):
        mask = used[...].astype(jnp.float32)
        mask_bf = mask.astype(jnp.bfloat16)
        mask_two = jnp.concatenate([mask_bf, mask_bf], 1)
        after = lax.rem(t + 1, tm)
        ext = jnp.concatenate(
            [xb[t], xb[after, :, :span], jnp.zeros((chans, LANES), jnp.bfloat16)], 1)
        for f in range(FRAMES):
            moved = ext[:, f * FINE : f * FINE + tile + span]
            for h in range(span // LANES):
                g = h * FRAMES + f
                fr[g * chans : (g + 1) * chans, :] = moved[:, h * LANES : h * LANES + wide]
        pr[...] = jnp.dot(ab[...], fr[...], preferred_element_type=jnp.float32)
        corr = pr[0:rows, :tile]
        for b in range(1, FINE):
            corr = corr + pltpu.roll(pr[b * rows : (b + 1) * rows, :], wide - b, 1)[:, :tile]
        x32 = ext[:, : tile + span].astype(jnp.float32)
        square = x32 * x32
        high = square.astype(jnp.bfloat16)
        low = (square - high.astype(jnp.float32)).astype(jnp.bfloat16)
        power = jnp.dot(mask_two, jnp.concatenate([high, low], 0),
                        preferred_element_type=jnp.float32)
        by = 1
        while by < span:
            power = power + pltpu.roll(power, tile + span - by, 1)
            by *= 2
        power = power[:, :tile]

        def put(ref, index):
            ref[index, 0:rows, 0:tile] = corr
            ref[index, rows : 2 * rows, 0:tile] = power
            ref[index, 0:rows, tile:] = tb[...]
            ref[index, rows : 2 * rows, tile:] = mask

        own = t % cs_n == my_at

        @pl.when(own)
        def _():
            put(rb, (blocks if extra else t // cs_n) * cs_n + my_cs)

        @pl.when(jnp.logical_not(own))
        def _():
            put(st, tm if extra else t)
            (extra_copy() if extra else sum_copy(t)).start()

    def step(u, carry):
        i = u // 2
        right_side = u % 2 == 0
        last = u == 2 * (tm - 1)
        from_left = me - 1 - i
        from_right = me + 1 + i
        first = jnp.logical_and(right_side, jnp.logical_not(last))

        left_ok = jnp.logical_and(first, from_left >= 0)
        right_ok = jnp.logical_and(first, from_right <= tm - 1)
        for p in range(PIECES):
            relay("wait_recv", x_ref, from_left, p, me, right_sem, left_ok)
            relay("start", xb.at[from_left], from_left, p, me + 1, right_sem,
                  jnp.logical_and(left_ok, me < tm - 1))
            relay("wait_recv", x_ref, from_right, p, me, left_sem, right_ok)
            relay("start", xb.at[from_right], from_right, p, me - 1, left_sem,
                  jnp.logical_and(right_ok, me > 0))

        @pl.when(jnp.logical_and(jnp.logical_and(first, i == tm - 3), is_helper))
        def _():
            for r in range(share):
                k = group * share + r
                wave_copy(k).wait_recv()
                for d in range(1, group_n):
                    swap_copy(k, d).start()

        t = jnp.where(last, tm - 1, jnp.where(right_side, me + i, from_left))
        valid = jnp.logical_or(
            last, jnp.logical_or(jnp.logical_and(right_side, from_right <= tm - 1),
                                 jnp.logical_and(jnp.logical_not(right_side), from_left >= 0)))

        @pl.when(jnp.logical_and(valid, jnp.logical_not(skipped(t))))
        def _():
            process(t, m_ref, False)

        return carry

    lax.fori_loop(0, 2 * (tm - 1) + 1, step, 0)

    @pl.when(is_helper)
    def _():
        mask_copy().wait_recv()
        for r in range(share, rows):
            wave_copy(lax.rem(group * share + r, rows)).wait_recv()
        prepare(wx, mx)
        process(extra_tile, mx, True)

    def reduced(q):
        for c in range(cs_n):
            @pl.when(my_cs != c)
            def _():
                pltpu.make_async_remote_copy(
                    src_ref=st.at[0], dst_ref=rb.at[q * cs_n + c], send_sem=out_sem.at[0],
                    recv_sem=in_sem.at[q * cs_n + c],
                    device_id={"tm": me}, device_id_type=MESH).wait_recv()
        total = rb[q * cs_n]
        for c in range(1, cs_n):
            total = total + rb[q * cs_n + c]
        te = jnp.sum(total[0:rows, tile:], axis=1, keepdims=True)
        active = jnp.sum(total[rows : 2 * rows, tile:], axis=1, keepdims=True)
        factor = jnp.sqrt(span * active)
        return (total[0:rows, :tile] * factor
                / jnp.sqrt(total[rows : 2 * rows, :tile] * te + EPSILON))

    def at_home(q):
        return jnp.logical_and(q * cs_n + my_at == me, my_cs == owner)

    for q in range(blocks):
        @pl.when(jnp.logical_not(skipped(q * cs_n + my_at)))
        def _():
            scores = reduced(q)

            @pl.when(at_home(q))
            def _():
                ob[me % blocks] = scores

            @pl.when(jnp.logical_not(at_home(q)))
            def _():
                fin[q] = scores
                score_copy(q).start()

    extra_here = jnp.logical_and(is_helper, extra_tile % cs_n == my_at)

    @pl.when(extra_here)
    def _():
        fin[blocks] = reduced(blocks)
        extra_score_copy().start()

    def finish(t, carry):
        for p in range(PIECES):
            relay("wait_send", x_ref, t, p, me + 1, right_sem,
                  jnp.logical_and(me < tm - 1, t <= me))
            relay("wait_send", x_ref, t, p, me - 1, left_sem, jnp.logical_and(me > 0, t >= me))

        @pl.when(jnp.logical_and(t % cs_n != my_at, jnp.logical_not(skipped(t))))
        def _():
            sum_copy(t).wait_send()

        return carry

    lax.fori_loop(0, tm, finish, 0)

    @pl.when(is_end)
    def _():
        mask_copy().wait_send()
        for k in range(share):
            wave_copy(group * share + k).wait_send()

    @pl.when(is_helper)
    def _():
        for r in range(share):
            for d in range(1, group_n):
                swap_copy(group * share + r, d).wait_send()

    @pl.when(jnp.logical_and(is_helper, extra_tile % cs_n != my_at))
    def _():
        extra_copy().wait_send()

    @pl.when(extra_here)
    def _():
        extra_score_copy().wait_send()

    for q in range(blocks):
        @pl.when(jnp.logical_not(jnp.logical_or(at_home(q), skipped(q * cs_n + my_at))))
        def _():
            score_copy(q).wait_send()

    for q in range(blocks):
        here = jnp.logical_and(my_cs * blocks + q == me, me % cs_n == my_at)

        @pl.when(jnp.logical_not(here))
        def _():
            pltpu.make_async_remote_copy(
                src_ref=fin.at[0], dst_ref=ob.at[q], send_sem=score_sem.at[0],
                recv_sem=done_sem.at[q],
                device_id={"tm": me}, device_id_type=MESH).wait_recv()
        o_ref[q * rows : (q + 1) * rows, :] = ob[q]


def solution(mesh):
    group_n, tm, chan_n, sub_n = (mesh.shape[a] for a in ("groups", "tm", "chan", "sub"))
    cs_n = chan_n * sub_n
    blocks = tm // cs_n

    def on_device(traces, templates, channel_mask):
        chans, tile = traces.shape
        rows, _, span = templates.shape
        coarse = span // FINE
        wide = tile + LANES
        vmem = pl.BlockSpec(memory_space=pltpu.VMEM)
        return pl.pallas_call(
            functools.partial(kernel, (group_n, tm, chan_n, sub_n)),
            out_shape=jax.ShapeDtypeStruct((blocks * rows, tile), jnp.float32),
            in_specs=[vmem] * 3,
            out_specs=vmem,
            scratch_shapes=[
                pltpu.VMEM((tm, chans, tile), jnp.bfloat16),
                pltpu.VMEM((coarse, FINE * rows, chans), jnp.float32),
                pltpu.VMEM((FINE * rows, coarse * chans), jnp.bfloat16),
                pltpu.VMEM((coarse * chans, wide), jnp.bfloat16),
                pltpu.VMEM((FINE * rows, wide), jnp.float32),
                pltpu.VMEM((tm + 1, 2 * rows, wide), jnp.float32),
                pltpu.VMEM((rows, chans), jnp.float32),
                pltpu.VMEM(((blocks + 1) * cs_n, 2 * rows, wide), jnp.float32),
                pltpu.VMEM((blocks + 1, rows, tile), jnp.float32),
                pltpu.VMEM((blocks, rows, tile), jnp.float32),
                pltpu.VMEM((rows, chans, span), jnp.bfloat16),
                pltpu.VMEM((rows, chans), jnp.int32),
                pltpu.SemaphoreType.DMA((tm, PIECES)),
                pltpu.SemaphoreType.DMA((tm, PIECES)),
                pltpu.SemaphoreType.DMA((tm, PIECES)),
                pltpu.SemaphoreType.DMA((tm + 1,)),
                pltpu.SemaphoreType.DMA(((blocks + 1) * cs_n,)),
                pltpu.SemaphoreType.DMA((blocks + 1,)),
                pltpu.SemaphoreType.DMA((blocks,)),
                pltpu.SemaphoreType.DMA((rows,)),
                pltpu.SemaphoreType.DMA((rows,)),
                pltpu.SemaphoreType.DMA((max(group_n - 1, 1), rows)),
                pltpu.SemaphoreType.DMA,
                pltpu.SemaphoreType.DMA,
            ],
            compiler_params=pltpu.CompilerParams(collective_id=0, has_side_effects=True),
        )(traces, templates, channel_mask)

    placed = (
        P(("chan", "sub"), ("groups", "tm")),
        P("tm", ("chan", "sub"), None),
        P("tm", ("chan", "sub")),
    )
    return jax.shard_map(
        on_device,
        mesh=mesh,
        in_specs=placed,
        out_specs=P(("chan", "sub"), ("groups", "tm")),
        check_vma=False,
    )
```

```python
import functools

import jax
import jax.numpy as jnp
from jax import lax
from jax.experimental import pallas as pl
from jax.experimental.pallas import tpu as pltpu
from jax.sharding import PartitionSpec as P

EPSILON = 1e-06
MESH = pl.DeviceIdType.MESH
LANES = 128
FRAMES = 4
FINE = LANES // FRAMES
PIECES = 2


def kernel(sizes, x_ref, w_ref, m_ref, o_ref, xb, af, ab, fr, pr, st, tb, rb, fin, ob,
           recv_sem, right_sem, left_sem, out_sem, in_sem, score_sem, done_sem):
    tm, chan_n, sub_n = sizes
    cs_n = chan_n * sub_n
    me = lax.axis_index("tm")
    my_chan = lax.axis_index("chan")
    my_sub = lax.axis_index("sub")
    my_cs = my_chan * sub_n + my_sub
    chans, tile = x_ref.shape
    rows, _, span = w_ref.shape
    blocks = tm // cs_n
    coarse = span // FINE
    reach = tile + LANES
    wide = tile + 2 * LANES
    owner = me // blocks
    my_at = my_sub * chan_n + my_chan

    def place(t):
        at = t % cs_n
        return at % chan_n, at // chan_n

    barrier = pltpu.get_barrier_semaphore()

    @pl.when(me < tm - 1)
    def _():
        pl.semaphore_signal(barrier, inc=1, device_id={"tm": me + 1}, device_id_type=MESH)

    @pl.when(me > 0)
    def _():
        pl.semaphore_signal(barrier, inc=1, device_id={"tm": me - 1}, device_id_type=MESH)

    for b in range(chan_n):
        for c in range(sub_n):
            if b or c:
                pl.semaphore_signal(
                    barrier, inc=1,
                    device_id={"chan": lax.rem(my_chan + b, chan_n),
                               "sub": lax.rem(my_sub + c, sub_n)},
                    device_id_type=MESH)

    xb[me] = x_ref[...]
    mask = m_ref[...].astype(jnp.float32)
    for k in range(rows):
        wave = jnp.transpose(w_ref[k].astype(jnp.float32)) * mask[k : k + 1, :]
        tb[k : k + 1, :] = jnp.sum(wave * wave, axis=0, keepdims=True)
        for g in range(coarse):
            af[g, pl.ds(k, FINE, stride=rows), :] = wave[g * FINE : (g + 1) * FINE, :]
    for g in range(coarse):
        ab[:, g * chans : (g + 1) * chans] = af[g].astype(jnp.bfloat16)
    mask_bf = mask.astype(jnp.bfloat16)
    mask_two = jnp.concatenate([mask_bf, mask_bf], 1)

    at_end = jnp.logical_or(me == 0, me == tm - 1)
    pl.semaphore_wait(barrier, cs_n - 1 + jnp.where(at_end, 1, 2))

    def relay(src, index, p, to, sem):
        columns = pl.ds(0, span) if p == 0 else pl.ds(span, tile - span)
        return pltpu.make_async_remote_copy(
            src_ref=src.at[:, columns], dst_ref=xb.at[index, :, columns],
            send_sem=sem.at[index, p], recv_sem=recv_sem.at[index, p],
            device_id={"tm": to}, device_id_type=MESH)

    for p in range(PIECES):
        @pl.when(me < tm - 1)
        def _():
            relay(x_ref, me, p, me + 1, right_sem).start()

        @pl.when(me > 0)
        def _():
            relay(x_ref, me, p, me - 1, left_sem).start()

    def sum_copy(t, kind):
        slot = (t // cs_n) * cs_n + my_cs
        to_chan, to_sub = place(t)
        part = (pl.ds(kind * rows, rows), pl.ds(0, wide if kind else tile))
        return pltpu.make_async_remote_copy(
            src_ref=st.at[(t, *part)], dst_ref=rb.at[(slot, *part)],
            send_sem=out_sem.at[t, kind], recv_sem=in_sem.at[slot, kind],
            device_id={"chan": to_chan, "sub": to_sub}, device_id_type=MESH)

    def score_copy(q):
        return pltpu.make_async_remote_copy(
            src_ref=fin.at[q], dst_ref=ob.at[me % blocks], send_sem=score_sem.at[q],
            recv_sem=done_sem.at[me % blocks],
            device_id={"tm": q * cs_n + my_at, "chan": owner // sub_n, "sub": owner % sub_n},
            device_id_type=MESH)

    def deliver(t, kind, fill):
        own = t % cs_n == my_at

        @pl.when(own)
        def _():
            fill(rb, (t // cs_n) * cs_n + my_cs)

        @pl.when(jnp.logical_not(own))
        def _():
            fill(st, t)
            sum_copy(t, kind).start()

    def process(t):
        after = lax.rem(t + 1, tm)
        ext = jnp.concatenate([xb[t], xb[after, :, :span]], 1)
        x32 = ext.astype(jnp.float32)
        square = x32 * x32
        high = square.astype(jnp.bfloat16)
        low = (square - high.astype(jnp.float32)).astype(jnp.bfloat16)
        power = jnp.dot(mask_two, jnp.concatenate([high, low], 0),
                        preferred_element_type=jnp.float32)
        by = 1
        while by < span:
            power = power + pltpu.roll(power, tile + span - by, 1)
            by *= 2

        def fill_power(ref, index):
            ref[index, rows : 2 * rows, 0:tile] = power[:, :tile]
            ref[index, rows : 2 * rows, tile : tile + LANES] = tb[...]
            ref[index, rows : 2 * rows, tile + LANES :] = mask

        deliver(t, 1, fill_power)
        ext = jnp.concatenate([ext, jnp.zeros((chans, LANES), jnp.bfloat16)], 1)
        for f in range(FRAMES):
            moved = ext[:, f * FINE : f * FINE + tile + span]
            for h in range(span // LANES):
                g = h * FRAMES + f
                fr[g * chans : (g + 1) * chans, :] = moved[:, h * LANES : h * LANES + reach]
        pr[...] = jnp.dot(ab[...], fr[...], preferred_element_type=jnp.float32)
        corr = pr[0:rows, :tile]
        for b in range(1, FINE):
            corr = corr + pltpu.roll(pr[b * rows : (b + 1) * rows, :], reach - b, 1)[:, :tile]

        def fill_corr(ref, index):
            ref[index, 0:rows, 0:tile] = corr

        deliver(t, 0, fill_corr)

    def step(u, carry):
        i = u // 2
        right_side = u % 2 == 0
        last = u == 2 * (tm - 1)
        from_left = me - 1 - i
        from_right = me + 1 + i
        for late in (False, True):
            here = jnp.logical_and(right_side != late, jnp.logical_not(last))
            for p in range(PIECES):
                if late and p == 0:
                    continue
                left_ok = jnp.logical_and(here, from_left >= 0)
                right_ok = jnp.logical_and(here, from_right <= tm - 1)
                if p:
                    left_ok = jnp.logical_and(left_ok, (me == tm - 1) == late)
                    right_ok = jnp.logical_and(right_ok, (me == 0) == late)

                @pl.when(left_ok)
                def _():
                    relay(x_ref, from_left, p, me, right_sem).wait_recv()

                    @pl.when(me < tm - 1)
                    def _():
                        relay(xb.at[from_left], from_left, p, me + 1, right_sem).start()

                @pl.when(right_ok)
                def _():
                    relay(x_ref, from_right, p, me, left_sem).wait_recv()

                    @pl.when(me > 0)
                    def _():
                        relay(xb.at[from_right], from_right, p, me - 1, left_sem).start()

        wrap = jnp.where(me == tm - 1, u == 2 * (tm - 2), last)
        t = jnp.where(wrap, tm - 1, jnp.where(right_side, me + i, from_left))
        valid = jnp.logical_or(
            wrap, jnp.logical_or(
                jnp.logical_and(jnp.logical_and(right_side, jnp.logical_not(last)),
                                from_right <= tm - 1),
                jnp.logical_and(jnp.logical_not(right_side), from_left >= 0)))

        @pl.when(valid)
        def _():
            process(t)

        return carry

    lax.fori_loop(0, 2 * (tm - 1) + 1, step, 0)

    for q in range(blocks):
        t = q * cs_n + my_at
        for c in range(cs_n):
            @pl.when(my_cs != c)
            def _():
                for kind in (1, 0):
                    part = (pl.ds(kind * rows, rows), pl.ds(0, wide if kind else tile))
                    pltpu.make_async_remote_copy(
                        src_ref=st.at[(0, *part)], dst_ref=rb.at[(q * cs_n + c, *part)],
                        send_sem=out_sem.at[0, kind], recv_sem=in_sem.at[q * cs_n + c, kind],
                        device_id={"tm": me}, device_id_type=MESH).wait_recv()

        def total(*at):
            result = rb[(q * cs_n, *at)]
            for c in range(1, cs_n):
                result = result + rb[(q * cs_n + c, *at)]
            return result

        lower, upper = slice(0, rows), slice(rows, 2 * rows)
        te = jnp.sum(total(upper, slice(tile, tile + LANES)), axis=1, keepdims=True)
        active = jnp.sum(total(upper, slice(tile + LANES, wide)), axis=1, keepdims=True)
        factor = jnp.sqrt(span * active)
        scores = (total(lower, slice(0, tile)) * factor
                  / jnp.sqrt(total(upper, slice(0, tile)) * te + EPSILON))
        here = jnp.logical_and(t == me, my_cs == owner)

        @pl.when(here)
        def _():
            ob[me % blocks] = scores

        @pl.when(jnp.logical_not(here))
        def _():
            fin[q] = scores
            score_copy(q).start()

    def finish(t, carry):
        for p in range(PIECES):
            @pl.when(jnp.logical_and(me < tm - 1, t <= me))
            def _():
                relay(x_ref, t, p, me, right_sem).wait_send()

            @pl.when(jnp.logical_and(me > 0, t >= me))
            def _():
                relay(x_ref, t, p, me, left_sem).wait_send()

        @pl.when(t % cs_n != my_at)
        def _():
            sum_copy(t, 1).wait_send()
            sum_copy(t, 0).wait_send()

        return carry

    lax.fori_loop(0, tm, finish, 0)

    for q in range(blocks):
        here = jnp.logical_and(q * cs_n + my_at == me, my_cs == owner)

        @pl.when(jnp.logical_not(here))
        def _():
            score_copy(q).wait_send()

    for q in range(blocks):
        here = jnp.logical_and(my_cs * blocks + q == me, me % cs_n == my_at)

        @pl.when(jnp.logical_not(here))
        def _():
            pltpu.make_async_remote_copy(
                src_ref=fin.at[0], dst_ref=ob.at[q], send_sem=score_sem.at[0],
                recv_sem=done_sem.at[q],
                device_id={"tm": me}, device_id_type=MESH).wait_recv()
        o_ref[q * rows : (q + 1) * rows, :] = ob[q]


def solution(mesh):
    tm, chan_n, sub_n = (mesh.shape[a] for a in ("tm", "chan", "sub"))
    cs_n = chan_n * sub_n
    blocks = tm // cs_n

    def on_device(traces, templates, channel_mask):
        chans, tile = traces.shape
        rows, _, span = templates.shape
        coarse = span // FINE
        reach = tile + LANES
        wide = tile + 2 * LANES
        vmem = pl.BlockSpec(memory_space=pltpu.VMEM)
        return pl.pallas_call(
            functools.partial(kernel, (tm, chan_n, sub_n)),
            out_shape=jax.ShapeDtypeStruct((blocks * rows, tile), jnp.float32),
            in_specs=[vmem] * 3,
            out_specs=vmem,
            scratch_shapes=[
                pltpu.VMEM((tm, chans, tile), jnp.bfloat16),
                pltpu.VMEM((coarse, FINE * rows, chans), jnp.float32),
                pltpu.VMEM((FINE * rows, coarse * chans), jnp.bfloat16),
                pltpu.VMEM((coarse * chans, reach), jnp.bfloat16),
                pltpu.VMEM((FINE * rows, reach), jnp.float32),
                pltpu.VMEM((tm, 2 * rows, wide), jnp.float32),
                pltpu.VMEM((rows, chans), jnp.float32),
                pltpu.VMEM((blocks * cs_n, 2 * rows, wide), jnp.float32),
                pltpu.VMEM((blocks, rows, tile), jnp.float32),
                pltpu.VMEM((blocks, rows, tile), jnp.float32),
                pltpu.SemaphoreType.DMA((tm, PIECES)),
                pltpu.SemaphoreType.DMA((tm, PIECES)),
                pltpu.SemaphoreType.DMA((tm, PIECES)),
                pltpu.SemaphoreType.DMA((tm, 2)),
                pltpu.SemaphoreType.DMA((blocks * cs_n, 2)),
                pltpu.SemaphoreType.DMA((blocks,)),
                pltpu.SemaphoreType.DMA((blocks,)),
            ],
            compiler_params=pltpu.CompilerParams(collective_id=0, has_side_effects=True),
        )(traces, templates, channel_mask)

    placed = (
        P(("chan", "sub"), ("groups", "tm")),
        P("tm", ("chan", "sub"), None),
        P("tm", ("chan", "sub")),
    )
    return jax.shard_map(
        on_device,
        mesh=mesh,
        in_specs=placed,
        out_specs=P(("chan", "sub"), ("groups", "tm")),
        check_vma=False,
    )
```

```python
import functools

import jax
import jax.numpy as jnp
from jax import lax
from jax.experimental import pallas as pl
from jax.experimental.pallas import tpu as pltpu
from jax.sharding import PartitionSpec as P

EPSILON = 1e-06
MESH = pl.DeviceIdType.MESH
LANES = 128
FRAMES = 4
FINE = LANES // FRAMES
PIECES = 2


def kernel(sizes, x_ref, w_ref, m_ref, o_ref, xb, af, ab, fr, pr, st, tb, rb, fin, ob,
           recv_sem, right_sem, left_sem, out_sem, in_sem, score_sem, done_sem):
    tm, chan_n, sub_n = sizes
    cs_n = chan_n * sub_n
    me = lax.axis_index("tm")
    my_chan = lax.axis_index("chan")
    my_sub = lax.axis_index("sub")
    my_cs = my_chan * sub_n + my_sub
    chans, tile = x_ref.shape
    rows, _, span = w_ref.shape
    blocks = tm // cs_n
    coarse = span // FINE
    reach = tile + LANES
    wide = tile + 2 * LANES
    owner = me // blocks
    my_at = cs_n - 1 - (my_sub * chan_n + my_chan)

    def place(t):
        at = cs_n - 1 - t % cs_n
        return at % chan_n, at // chan_n

    barrier = pltpu.get_barrier_semaphore()

    @pl.when(me < tm - 1)
    def _():
        pl.semaphore_signal(barrier, inc=1, device_id={"tm": me + 1}, device_id_type=MESH)

    @pl.when(me > 0)
    def _():
        pl.semaphore_signal(barrier, inc=1, device_id={"tm": me - 1}, device_id_type=MESH)

    for b in range(chan_n):
        for c in range(sub_n):
            if b or c:
                pl.semaphore_signal(
                    barrier, inc=1,
                    device_id={"chan": lax.rem(my_chan + b, chan_n),
                               "sub": lax.rem(my_sub + c, sub_n)},
                    device_id_type=MESH)

    xb[me] = x_ref[...]
    mask = m_ref[...].astype(jnp.float32)
    for k in range(rows):
        wave = jnp.transpose(w_ref[k].astype(jnp.float32)) * mask[k : k + 1, :]
        tb[k : k + 1, :] = jnp.sum(wave * wave, axis=0, keepdims=True)
        for g in range(coarse):
            af[g, pl.ds(k, FINE, stride=rows), :] = wave[g * FINE : (g + 1) * FINE, :]
    for g in range(coarse):
        ab[:, g * chans : (g + 1) * chans] = af[g].astype(jnp.bfloat16)
    mask_bf = mask.astype(jnp.bfloat16)
    mask_two = jnp.concatenate([mask_bf, mask_bf], 1)

    at_end = jnp.logical_or(me == 0, me == tm - 1)
    pl.semaphore_wait(barrier, cs_n - 1 + jnp.where(at_end, 1, 2))

    def relay(src, index, p, to, sem):
        columns = pl.ds(0, span) if p == 0 else pl.ds(span, tile - span)
        return pltpu.make_async_remote_copy(
            src_ref=src.at[:, columns], dst_ref=xb.at[index, :, columns],
            send_sem=sem.at[index, p], recv_sem=recv_sem.at[index, p],
            device_id={"tm": to}, device_id_type=MESH)

    for p in range(PIECES):
        @pl.when(me < tm - 1)
        def _():
            relay(x_ref, me, p, me + 1, right_sem).start()

        @pl.when(me > 0)
        def _():
            relay(x_ref, me, p, me - 1, left_sem).start()

    def sum_copy(t, kind):
        slot = (t // cs_n) * cs_n + my_cs
        to_chan, to_sub = place(t)
        part = (pl.ds(kind * rows, rows), pl.ds(0, wide if kind else tile))
        return pltpu.make_async_remote_copy(
            src_ref=st.at[(t, *part)], dst_ref=rb.at[(slot, *part)],
            send_sem=out_sem.at[t, kind], recv_sem=in_sem.at[slot, kind],
            device_id={"chan": to_chan, "sub": to_sub}, device_id_type=MESH)

    def score_copy(q):
        return pltpu.make_async_remote_copy(
            src_ref=fin.at[q], dst_ref=ob.at[me % blocks], send_sem=score_sem.at[q],
            recv_sem=done_sem.at[me % blocks],
            device_id={"tm": q * cs_n + my_at, "chan": owner // sub_n, "sub": owner % sub_n},
            device_id_type=MESH)

    def deliver(t, kind, fill):
        own = t % cs_n == my_at

        @pl.when(own)
        def _():
            fill(rb, (t // cs_n) * cs_n + my_cs)

        @pl.when(jnp.logical_not(own))
        def _():
            fill(st, t)
            sum_copy(t, kind).start()

    def process(t):
        after = lax.rem(t + 1, tm)
        ext = jnp.concatenate([xb[t], xb[after, :, :span]], 1)
        x32 = ext.astype(jnp.float32)
        square = x32 * x32
        high = square.astype(jnp.bfloat16)
        low = (square - high.astype(jnp.float32)).astype(jnp.bfloat16)
        power = jnp.dot(mask_two, jnp.concatenate([high, low], 0),
                        preferred_element_type=jnp.float32)
        by = 1
        while by < span:
            power = power + pltpu.roll(power, tile + span - by, 1)
            by *= 2

        def fill_power(ref, index):
            ref[index, rows : 2 * rows, 0:tile] = power[:, :tile]
            ref[index, rows : 2 * rows, tile : tile + LANES] = tb[...]
            ref[index, rows : 2 * rows, tile + LANES :] = mask

        deliver(t, 1, fill_power)
        ext = jnp.concatenate([ext, jnp.zeros((chans, LANES), jnp.bfloat16)], 1)
        for f in range(FRAMES):
            moved = ext[:, f * FINE : f * FINE + tile + span]
            for h in range(span // LANES):
                g = h * FRAMES + f
                fr[g * chans : (g + 1) * chans, :] = moved[:, h * LANES : h * LANES + reach]
        pr[...] = jnp.dot(ab[...], fr[...], preferred_element_type=jnp.float32)
        corr = pr[0:rows, :tile]
        for b in range(1, FINE):
            corr = corr + pltpu.roll(pr[b * rows : (b + 1) * rows, :], reach - b, 1)[:, :tile]

        def fill_corr(ref, index):
            ref[index, 0:rows, 0:tile] = corr

        deliver(t, 0, fill_corr)

    def step(u, carry):
        i = u // 2
        right_side = u % 2 == 0
        last = u == 2 * (tm - 1)
        from_left = me - 1 - i
        from_right = me + 1 + i
        for late in (False, True):
            here = jnp.logical_and(right_side != late, jnp.logical_not(last))
            for p in range(PIECES):
                if late and p == 0:
                    continue
                left_ok = jnp.logical_and(here, from_left >= 0)
                right_ok = jnp.logical_and(here, from_right <= tm - 1)
                if p:
                    left_ok = jnp.logical_and(left_ok, (me == tm - 1) == late)
                    right_ok = jnp.logical_and(right_ok, (me == 0) == late)

                @pl.when(left_ok)
                def _():
                    relay(x_ref, from_left, p, me, right_sem).wait_recv()

                    @pl.when(me < tm - 1)
                    def _():
                        relay(xb.at[from_left], from_left, p, me + 1, right_sem).start()

                @pl.when(right_ok)
                def _():
                    relay(x_ref, from_right, p, me, left_sem).wait_recv()

                    @pl.when(me > 0)
                    def _():
                        relay(xb.at[from_right], from_right, p, me - 1, left_sem).start()

        wrap = jnp.where(me == tm - 1, u == 2 * (tm - 2), last)
        t = jnp.where(wrap, tm - 1, jnp.where(right_side, me + i, from_left))
        valid = jnp.logical_or(
            wrap, jnp.logical_or(
                jnp.logical_and(jnp.logical_and(right_side, jnp.logical_not(last)),
                                from_right <= tm - 1),
                jnp.logical_and(jnp.logical_not(right_side), from_left >= 0)))

        @pl.when(valid)
        def _():
            process(t)

        return carry

    lax.fori_loop(0, 2 * (tm - 1) + 1, step, 0)

    for q in range(blocks):
        t = q * cs_n + my_at
        for c in range(cs_n):
            @pl.when(my_cs != c)
            def _():
                for kind in (1, 0):
                    part = (pl.ds(kind * rows, rows), pl.ds(0, wide if kind else tile))
                    pltpu.make_async_remote_copy(
                        src_ref=st.at[(0, *part)], dst_ref=rb.at[(q * cs_n + c, *part)],
                        send_sem=out_sem.at[0, kind], recv_sem=in_sem.at[q * cs_n + c, kind],
                        device_id={"tm": me}, device_id_type=MESH).wait_recv()

        def total(*at):
            result = rb[(q * cs_n, *at)]
            for c in range(1, cs_n):
                result = result + rb[(q * cs_n + c, *at)]
            return result

        lower, upper = slice(0, rows), slice(rows, 2 * rows)
        te = jnp.sum(total(upper, slice(tile, tile + LANES)), axis=1, keepdims=True)
        active = jnp.sum(total(upper, slice(tile + LANES, wide)), axis=1, keepdims=True)
        factor = jnp.sqrt(span * active)
        scores = (total(lower, slice(0, tile)) * factor
                  / jnp.sqrt(total(upper, slice(0, tile)) * te + EPSILON))
        here = jnp.logical_and(t == me, my_cs == owner)

        @pl.when(here)
        def _():
            ob[me % blocks] = scores

        @pl.when(jnp.logical_not(here))
        def _():
            fin[q] = scores
            score_copy(q).start()

    def finish(t, carry):
        for p in range(PIECES):
            @pl.when(jnp.logical_and(me < tm - 1, t <= me))
            def _():
                relay(x_ref, t, p, me, right_sem).wait_send()

            @pl.when(jnp.logical_and(me > 0, t >= me))
            def _():
                relay(x_ref, t, p, me, left_sem).wait_send()

        @pl.when(t % cs_n != my_at)
        def _():
            sum_copy(t, 1).wait_send()
            sum_copy(t, 0).wait_send()

        return carry

    lax.fori_loop(0, tm, finish, 0)

    for q in range(blocks):
        here = jnp.logical_and(q * cs_n + my_at == me, my_cs == owner)

        @pl.when(jnp.logical_not(here))
        def _():
            score_copy(q).wait_send()

    for q in range(blocks):
        here = jnp.logical_and(my_cs * blocks + q == me, me % cs_n == my_at)

        @pl.when(jnp.logical_not(here))
        def _():
            pltpu.make_async_remote_copy(
                src_ref=fin.at[0], dst_ref=ob.at[q], send_sem=score_sem.at[0],
                recv_sem=done_sem.at[q],
                device_id={"tm": me}, device_id_type=MESH).wait_recv()
        o_ref[q * rows : (q + 1) * rows, :] = ob[q]


def solution(mesh):
    tm, chan_n, sub_n = (mesh.shape[a] for a in ("tm", "chan", "sub"))
    cs_n = chan_n * sub_n
    blocks = tm // cs_n

    def on_device(traces, templates, channel_mask):
        chans, tile = traces.shape
        rows, _, span = templates.shape
        coarse = span // FINE
        reach = tile + LANES
        wide = tile + 2 * LANES
        vmem = pl.BlockSpec(memory_space=pltpu.VMEM)
        return pl.pallas_call(
            functools.partial(kernel, (tm, chan_n, sub_n)),
            out_shape=jax.ShapeDtypeStruct((blocks * rows, tile), jnp.float32),
            in_specs=[vmem] * 3,
            out_specs=vmem,
            scratch_shapes=[
                pltpu.VMEM((tm, chans, tile), jnp.bfloat16),
                pltpu.VMEM((coarse, FINE * rows, chans), jnp.float32),
                pltpu.VMEM((FINE * rows, coarse * chans), jnp.bfloat16),
                pltpu.VMEM((coarse * chans, reach), jnp.bfloat16),
                pltpu.VMEM((FINE * rows, reach), jnp.float32),
                pltpu.VMEM((tm, 2 * rows, wide), jnp.float32),
                pltpu.VMEM((rows, chans), jnp.float32),
                pltpu.VMEM((blocks * cs_n, 2 * rows, wide), jnp.float32),
                pltpu.VMEM((blocks, rows, tile), jnp.float32),
                pltpu.VMEM((blocks, rows, tile), jnp.float32),
                pltpu.SemaphoreType.DMA((tm, PIECES)),
                pltpu.SemaphoreType.DMA((tm, PIECES)),
                pltpu.SemaphoreType.DMA((tm, PIECES)),
                pltpu.SemaphoreType.DMA((tm, 2)),
                pltpu.SemaphoreType.DMA((blocks * cs_n, 2)),
                pltpu.SemaphoreType.DMA((blocks,)),
                pltpu.SemaphoreType.DMA((blocks,)),
            ],
            compiler_params=pltpu.CompilerParams(collective_id=0, has_side_effects=True),
        )(traces, templates, channel_mask)

    placed = (
        P(("chan", "sub"), ("groups", "tm")),
        P("tm", ("chan", "sub"), None),
        P("tm", ("chan", "sub")),
    )
    return jax.shard_map(
        on_device,
        mesh=mesh,
        in_specs=placed,
        out_specs=P(("chan", "sub"), ("groups", "tm")),
        check_vma=False,
    )
```

```python
import functools

import jax
import jax.numpy as jnp
from jax import lax
from jax.experimental import pallas as pl
from jax.experimental.pallas import tpu as pltpu
from jax.sharding import PartitionSpec as P

EPSILON = 1e-06
MESH = pl.DeviceIdType.MESH
LANES = 128
FRAMES = 4
FINE = LANES // FRAMES
PIECES = 2


def kernel(sizes, x_ref, w_ref, m_ref, o_ref, xb, af, ab, fr, pr, st, tb, rb, fin, ob,
           recv_sem, right_sem, left_sem, out_sem, in_sem, score_sem, done_sem):
    tm, chan_n, sub_n = sizes
    cs_n = chan_n * sub_n
    me = lax.axis_index("tm")
    my_chan = lax.axis_index("chan")
    my_sub = lax.axis_index("sub")
    my_cs = my_chan * sub_n + my_sub
    chans, tile = x_ref.shape
    rows, _, span = w_ref.shape
    blocks = tm // cs_n
    coarse = span // FINE
    reach = tile + LANES
    wide = tile + 2 * LANES
    owner = me // blocks
    my_at = cs_n - 1 - (my_sub * chan_n + my_chan)

    def place(t):
        at = cs_n - 1 - t % cs_n
        return at % chan_n, at // chan_n

    barrier = pltpu.get_barrier_semaphore()

    @pl.when(me < tm - 1)
    def _():
        pl.semaphore_signal(barrier, inc=1, device_id={"tm": me + 1}, device_id_type=MESH)

    @pl.when(me > 0)
    def _():
        pl.semaphore_signal(barrier, inc=1, device_id={"tm": me - 1}, device_id_type=MESH)

    for b in range(chan_n):
        for c in range(sub_n):
            if b or c:
                pl.semaphore_signal(
                    barrier, inc=1,
                    device_id={"chan": lax.rem(my_chan + b, chan_n),
                               "sub": lax.rem(my_sub + c, sub_n)},
                    device_id_type=MESH)

    xb[me] = x_ref[...]
    mask = m_ref[...].astype(jnp.float32)
    for k in range(rows):
        wave = jnp.transpose(w_ref[k].astype(jnp.float32)) * mask[k : k + 1, :]
        tb[k : k + 1, :] = jnp.sum(wave * wave, axis=0, keepdims=True)
        for g in range(coarse):
            af[g, pl.ds(k, FINE, stride=rows), :] = wave[g * FINE : (g + 1) * FINE, :]
    for g in range(coarse):
        ab[:, g * chans : (g + 1) * chans] = af[g].astype(jnp.bfloat16)
    mask_bf = mask.astype(jnp.bfloat16)
    mask_two = jnp.concatenate([mask_bf, mask_bf], 1)

    at_end = jnp.logical_or(me == 0, me == tm - 1)
    pl.semaphore_wait(barrier, cs_n - 1 + jnp.where(at_end, 1, 2))

    def relay(src, index, p, to, sem):
        columns = pl.ds(0, span) if p == 0 else pl.ds(span, tile - span)
        return pltpu.make_async_remote_copy(
            src_ref=src.at[:, columns], dst_ref=xb.at[index, :, columns],
            send_sem=sem.at[index, p], recv_sem=recv_sem.at[index, p],
            device_id={"tm": to}, device_id_type=MESH)

    for p in range(PIECES):
        @pl.when(me < tm - 1)
        def _():
            relay(x_ref, me, p, me + 1, right_sem).start()

        @pl.when(me > 0)
        def _():
            relay(x_ref, me, p, me - 1, left_sem).start()

    def sum_copy(t, kind):
        slot = (t // cs_n) * cs_n + my_cs
        to_chan, to_sub = place(t)
        part = (pl.ds(kind * rows, rows), pl.ds(0, wide if kind else tile))
        return pltpu.make_async_remote_copy(
            src_ref=st.at[(t, *part)], dst_ref=rb.at[(slot, *part)],
            send_sem=out_sem.at[t, kind], recv_sem=in_sem.at[slot, kind],
            device_id={"chan": to_chan, "sub": to_sub}, device_id_type=MESH)

    def score_copy(q):
        return pltpu.make_async_remote_copy(
            src_ref=fin.at[q], dst_ref=ob.at[me % blocks], send_sem=score_sem.at[q],
            recv_sem=done_sem.at[me % blocks],
            device_id={"tm": q * cs_n + my_at, "chan": owner // sub_n, "sub": owner % sub_n},
            device_id_type=MESH)

    def deliver(t, kind, fill):
        own = t % cs_n == my_at

        @pl.when(own)
        def _():
            fill(rb, (t // cs_n) * cs_n + my_cs)

        @pl.when(jnp.logical_not(own))
        def _():
            fill(st, t)
            sum_copy(t, kind).start()

    def process(t):
        after = lax.rem(t + 1, tm)
        ext = jnp.concatenate([xb[t], xb[after, :, :span]], 1)
        x32 = ext.astype(jnp.float32)
        square = x32 * x32
        high = square.astype(jnp.bfloat16)
        low = (square - high.astype(jnp.float32)).astype(jnp.bfloat16)
        power = jnp.dot(mask_two, jnp.concatenate([high, low], 0),
                        preferred_element_type=jnp.float32)
        by = 1
        while by < span:
            power = power + pltpu.roll(power, tile + span - by, 1)
            by *= 2

        def fill_power(ref, index):
            ref[index, rows : 2 * rows, 0:tile] = power[:, :tile]
            ref[index, rows : 2 * rows, tile : tile + LANES] = tb[...]
            ref[index, rows : 2 * rows, tile + LANES :] = mask

        deliver(t, 1, fill_power)
        ext = jnp.concatenate([ext, jnp.zeros((chans, LANES), jnp.bfloat16)], 1)
        for f in range(FRAMES):
            moved = ext[:, f * FINE : f * FINE + tile + span]
            for h in range(span // LANES):
                g = h * FRAMES + f
                fr[g * chans : (g + 1) * chans, :] = moved[:, h * LANES : h * LANES + reach]
        pr[...] = jnp.dot(ab[...], fr[...], preferred_element_type=jnp.float32)
        corr = pr[0:rows, :tile]
        for b in range(1, FINE):
            corr = corr + pltpu.roll(pr[b * rows : (b + 1) * rows, :], reach - b, 1)[:, :tile]

        def fill_corr(ref, index):
            ref[index, 0:rows, 0:tile] = corr

        deliver(t, 0, fill_corr)

    def step(u, carry):
        i = u // 2
        right_side = u % 2 == 0
        last = u == 2 * (tm - 1)
        from_left = me - 1 - i
        from_right = me + 1 + i
        for late in (False, True):
            here = jnp.logical_and(right_side != late, jnp.logical_not(last))
            for p in range(PIECES):
                if late and p == 0:
                    continue
                left_ok = jnp.logical_and(here, from_left >= 0)
                right_ok = jnp.logical_and(here, from_right <= tm - 1)
                if p:
                    left_ok = jnp.logical_and(left_ok, (me == tm - 1) == late)
                    right_ok = jnp.logical_and(right_ok, (me == 0) == late)

                @pl.when(left_ok)
                def _():
                    relay(x_ref, from_left, p, me, right_sem).wait_recv()

                    @pl.when(me < tm - 1)
                    def _():
                        relay(xb.at[from_left], from_left, p, me + 1, right_sem).start()

                @pl.when(right_ok)
                def _():
                    relay(x_ref, from_right, p, me, left_sem).wait_recv()

                    @pl.when(me > 0)
                    def _():
                        relay(xb.at[from_right], from_right, p, me - 1, left_sem).start()

        wrap = jnp.where(me == tm - 1, u == 2 * (tm - 2), last)
        t = jnp.where(wrap, tm - 1, jnp.where(right_side, me + i, from_left))
        valid = jnp.logical_or(
            wrap, jnp.logical_or(
                jnp.logical_and(jnp.logical_and(right_side, jnp.logical_not(last)),
                                from_right <= tm - 1),
                jnp.logical_and(jnp.logical_not(right_side), from_left >= 0)))

        @pl.when(valid)
        def _():
            process(t)

        return carry

    lax.fori_loop(0, 2 * (tm - 1) + 1, step, 0)

    for q in range(blocks):
        t = q * cs_n + my_at
        def arrive(kind):
            part = (pl.ds(kind * rows, rows), pl.ds(0, wide if kind else tile))
            for c in range(cs_n):
                @pl.when(my_cs != c)
                def _():
                    pltpu.make_async_remote_copy(
                        src_ref=st.at[(0, *part)], dst_ref=rb.at[(q * cs_n + c, *part)],
                        send_sem=out_sem.at[0, kind], recv_sem=in_sem.at[q * cs_n + c, kind],
                        device_id={"tm": me}, device_id_type=MESH).wait_recv()

        arrive(1)

        def total(*at):
            result = rb[(q * cs_n, *at)]
            for c in range(1, cs_n):
                result = result + rb[(q * cs_n + c, *at)]
            return result

        lower, upper = slice(0, rows), slice(rows, 2 * rows)
        te = jnp.sum(total(upper, slice(tile, tile + LANES)), axis=1, keepdims=True)
        active = jnp.sum(total(upper, slice(tile + LANES, wide)), axis=1, keepdims=True)
        factor = jnp.sqrt(span * active)
        root = jnp.sqrt(total(upper, slice(0, tile)) * te + EPSILON)
        arrive(0)
        scores = total(lower, slice(0, tile)) * factor / root
        here = jnp.logical_and(t == me, my_cs == owner)

        @pl.when(here)
        def _():
            ob[me % blocks] = scores

        @pl.when(jnp.logical_not(here))
        def _():
            fin[q] = scores
            score_copy(q).start()

    def finish(t, carry):
        for p in range(PIECES):
            @pl.when(jnp.logical_and(me < tm - 1, t <= me))
            def _():
                relay(x_ref, t, p, me, right_sem).wait_send()

            @pl.when(jnp.logical_and(me > 0, t >= me))
            def _():
                relay(x_ref, t, p, me, left_sem).wait_send()

        @pl.when(t % cs_n != my_at)
        def _():
            sum_copy(t, 1).wait_send()
            sum_copy(t, 0).wait_send()

        return carry

    lax.fori_loop(0, tm, finish, 0)

    for q in range(blocks):
        here = jnp.logical_and(q * cs_n + my_at == me, my_cs == owner)

        @pl.when(jnp.logical_not(here))
        def _():
            score_copy(q).wait_send()

    for q in range(blocks):
        here = jnp.logical_and(my_cs * blocks + q == me, me % cs_n == my_at)

        @pl.when(jnp.logical_not(here))
        def _():
            pltpu.make_async_remote_copy(
                src_ref=fin.at[0], dst_ref=ob.at[q], send_sem=score_sem.at[0],
                recv_sem=done_sem.at[q],
                device_id={"tm": me}, device_id_type=MESH).wait_recv()
        o_ref[q * rows : (q + 1) * rows, :] = ob[q]


def solution(mesh):
    tm, chan_n, sub_n = (mesh.shape[a] for a in ("tm", "chan", "sub"))
    cs_n = chan_n * sub_n
    blocks = tm // cs_n

    def on_device(traces, templates, channel_mask):
        chans, tile = traces.shape
        rows, _, span = templates.shape
        coarse = span // FINE
        reach = tile + LANES
        wide = tile + 2 * LANES
        vmem = pl.BlockSpec(memory_space=pltpu.VMEM)
        return pl.pallas_call(
            functools.partial(kernel, (tm, chan_n, sub_n)),
            out_shape=jax.ShapeDtypeStruct((blocks * rows, tile), jnp.float32),
            in_specs=[vmem] * 3,
            out_specs=vmem,
            scratch_shapes=[
                pltpu.VMEM((tm, chans, tile), jnp.bfloat16),
                pltpu.VMEM((coarse, FINE * rows, chans), jnp.float32),
                pltpu.VMEM((FINE * rows, coarse * chans), jnp.bfloat16),
                pltpu.VMEM((coarse * chans, reach), jnp.bfloat16),
                pltpu.VMEM((FINE * rows, reach), jnp.float32),
                pltpu.VMEM((tm, 2 * rows, wide), jnp.float32),
                pltpu.VMEM((rows, chans), jnp.float32),
                pltpu.VMEM((blocks * cs_n, 2 * rows, wide), jnp.float32),
                pltpu.VMEM((blocks, rows, tile), jnp.float32),
                pltpu.VMEM((blocks, rows, tile), jnp.float32),
                pltpu.SemaphoreType.DMA((tm, PIECES)),
                pltpu.SemaphoreType.DMA((tm, PIECES)),
                pltpu.SemaphoreType.DMA((tm, PIECES)),
                pltpu.SemaphoreType.DMA((tm, 2)),
                pltpu.SemaphoreType.DMA((blocks * cs_n, 2)),
                pltpu.SemaphoreType.DMA((blocks,)),
                pltpu.SemaphoreType.DMA((blocks,)),
            ],
            compiler_params=pltpu.CompilerParams(collective_id=0, has_side_effects=True),
        )(traces, templates, channel_mask)

    placed = (
        P(("chan", "sub"), ("groups", "tm")),
        P("tm", ("chan", "sub"), None),
        P("tm", ("chan", "sub")),
    )
    return jax.shard_map(
        on_device,
        mesh=mesh,
        in_specs=placed,
        out_specs=P(("chan", "sub"), ("groups", "tm")),
        check_vma=False,
    )
```
